256 devices in a mesh: coil: 8 (over z_hi, x), ro: 32 (over y, z_lo, core).
Axes of the slice: x: 4, y: 4, z: 8 (z_hi: 2, z_lo: 4; z = z_hi * 4 + z_lo), core: 2. Of those that a mesh axis runs over, the one named last changes fastest.
Arguments:
- kspace: bfloat16 [2, 64, 32, 448, 320], P(None, 'coil', None, 'ro'), may hold values from -884272563206990856199 to 884272563206990856199
- sensitivity: bfloat16 [2, 64, 32, 448, 320], P(None, 'coil', 'ro'), may hold values from -0.75 to 0.75
- sampled: int32 [32, 448], replicated, may hold values 0 or 1
- pole_y: int32 [32, 320], replicated, may hold values from 4 to 112
- order_y: int32 [32, 320], replicated, may hold values from 1 to 3
- pole_z: int32 [32, 448], replicated, may hold values from 4 to 80
- order_z: int32 [32, 448], replicated, may hold values from 1 to 3
Outputs:
- image: float32 [2, 32, 448, 320], P(None, 'ro', 'coil')
The draws below stay inside these ranges and needn't reach their ends.
All inputs are finite; a program needn't handle non-finite values.
Results may differ from the reference program's by a relative error of at most 0.0056.
Values may be sent and summed in bfloat16 or wider, within the bound.
A program may use at most 128 MiB of HBM per device.

```python
import math
import jax
import jax.numpy as jnp
from jax import lax

C = 64
KY = 448
KZ = 320
RO = 32


def window_params(key):
    pole_rows = jax.random.randint(jax.random.fold_in(key, 101), (RO, KZ), 4, KY // 4 + 1, dtype=jnp.int32)
    order_rows = jax.random.randint(jax.random.fold_in(key, 102), (RO, KZ), 1, 4, dtype=jnp.int32)
    pole_cols = jax.random.randint(jax.random.fold_in(key, 103), (RO, KY), 4, KZ // 4 + 1, dtype=jnp.int32)
    order_cols = jax.random.randint(jax.random.fold_in(key, 104), (RO, KY), 1, 4, dtype=jnp.int32)
    return (pole_rows, order_rows, pole_cols, order_cols)


def draw_pole_y(key, part):
    return window_params(key)[0]


def draw_order_y(key, part):
    return window_params(key)[1]


def draw_pole_z(key, part):
    return window_params(key)[2]


def draw_order_z(key, part):
    return window_params(key)[3]


def draw_kspace(key, part):
    pole_rows, order_rows, pole_cols, order_cols = window_params(key)
    index_y = jnp.arange(KY, dtype=jnp.int32)
    freq_y = jnp.minimum(index_y, KY - index_y).astype(jnp.float32)
    index_z = jnp.arange(KZ, dtype=jnp.int32)
    freq_z = jnp.minimum(index_z, KZ - index_z).astype(jnp.float32)
    ratio_y = freq_y[None, :, None] / pole_rows[:, None, :].astype(jnp.float32)
    growth_y = 1.0 + jnp.power(ratio_y, 2.0 * order_rows[:, None, :].astype(jnp.float32))
    ratio_z = freq_z[None, None, :] / pole_cols[:, :, None].astype(jnp.float32)
    growth_z = 1.0 + jnp.power(ratio_z, 2.0 * order_cols[:, :, None].astype(jnp.float32))
    noise_key = jax.random.fold_in(key, 111)
    values = jnp.clip(jax.random.normal(noise_key, (2, C, RO, KY, KZ), jnp.float32), -6.0, 6.0)
    return (values * (growth_y * growth_z)[None, None]).astype(jnp.bfloat16)


def with_ends(array, key, smallest, top_value):
    dims = array.shape
    place = [jax.random.randint(jax.random.fold_in(key, axis), (), 0, dims[axis]) for axis in range(len(dims))]
    array = array.at[tuple(place)].set(smallest)
    longest = dims.index(max(dims))
    place[longest] = (place[longest] + 1) % dims[longest]
    return array.at[tuple(place)].set(top_value)


def raised(entries, own_key, source, target, shards_of, factor):
    owner, partner = [(jnp.arange(entries.shape[position]) // (entries.shape[position] // shards_of)).reshape([-1 if axis == position else 1 for axis in range(entries.ndim)]) for position in (source, target)]
    chosen = jax.random.permutation(own_key, shards_of)[partner]
    strong = (owner == chosen) | (owner == (partner + shards_of // 2) % shards_of)
    return jnp.where(strong, factor * entries, entries)


def levels(own_key, extent, cuts, least, top_value):
    loudness = 1.0
    for axis_at, blocks in cuts:
        draws = jax.random.uniform(jax.random.fold_in(jax.random.fold_in(own_key, 6), axis_at), (blocks,), jnp.float32, least / len(cuts), top_value / len(cuts))
        loudness = loudness * jnp.repeat(jnp.exp(draws), extent[axis_at] // blocks).reshape((-1,) + (1,) * (len(extent) - 1 - axis_at))
    return loudness


def noise_with(key, shape, spread, reach, shards, heavy, kind=jnp.bfloat16):
    result = spread * jax.random.normal(key, shape, jnp.float32)
    if shards:
        result = result * levels(key, shape, shards, -0.22, 0.18)
    return jnp.clip(raised(result, jax.random.fold_in(key, 3), *heavy), -reach, reach).astype(kind)


def setup_inputs(seed: int = 0) -> dict:
    key_list = jax.random.split(jax.random.key(seed), 8)
    return {
        "kspace": draw_kspace(jax.random.fold_in(key_list[7], 71), 0),
        "sensitivity": noise_with(key_list[1], (2, C, RO, KY, KZ), (2 * C) ** -0.5, 0.75, ((1, 8), (2, 32)), (1, 3, 8, 2.0)),
        "sampled": with_ends((jax.random.randint(key_list[2], (RO, KY), 0, 4) < 3).astype(jnp.int32), jax.random.fold_in(key_list[2], 1), 0, 1),
        "pole_y": draw_pole_y(jax.random.fold_in(key_list[7], 71), 0),
        "order_y": draw_order_y(jax.random.fold_in(key_list[7], 71), 0),
        "pole_z": draw_pole_z(jax.random.fold_in(key_list[7], 71), 0),
        "order_z": draw_order_z(jax.random.fold_in(key_list[7], 71), 0),
    }


def dft_tables(length):
    index = jnp.arange(length, dtype=jnp.int32)
    product = index[:, None] * index[None, :] % length
    angle = product.astype(jnp.float32) * (2.0 * math.pi / length)
    factor = 1.0 / math.sqrt(length)
    return ((jnp.cos(angle) * factor).astype(jnp.bfloat16), (jnp.sin(angle) * factor).astype(jnp.bfloat16))

def line_window(frequency, pole, degree):
    quotient = frequency / pole.astype(jnp.float32)
    return 1.0 / (1.0 + jnp.power(quotient, 2.0 * degree.astype(jnp.float32)))

def fold_freq(length):
    index = jnp.arange(length, dtype=jnp.int32)
    return jnp.minimum(index, length - index).astype(jnp.float32)

def reference(kspace, sensitivity, sampled, pole_y, order_y, pole_z, order_z):
    kz_cosine, kz_sine = dft_tables(KZ)
    ky_cosine, ky_sine = dft_tables(KY)
    freq_y = fold_freq(KY)
    freq_z = fold_freq(KZ)
    high = lax.Precision.HIGHEST

    def recon_one(readout):
        block = lax.dynamic_index_in_dim(kspace, readout, 2, keepdims=False)
        maps = lax.dynamic_index_in_dim(sensitivity, readout, 2, keepdims=False).astype(jnp.float32)
        weight_y = sampled[readout][:, None].astype(jnp.float32) * line_window(freq_y[:, None], pole_y[readout][None, :], order_y[readout][None, :])
        weight_z = line_window(freq_z[None, :], pole_z[readout][:, None], order_z[readout][:, None])
        filtered = (block.astype(jnp.float32) * weight_y * weight_z).astype(jnp.bfloat16).astype(jnp.float32)
        real_part, imag_part = (filtered[0], filtered[1])
        cos_z = kz_cosine.astype(jnp.float32)
        sin_z = kz_sine.astype(jnp.float32)
        hyb_real = jnp.einsum('ckz,zn->ckn', real_part, cos_z, precision=high) - jnp.einsum('ckz,zn->ckn', imag_part, sin_z, precision=high)
        hyb_imag = jnp.einsum('ckz,zn->ckn', real_part, sin_z, precision=high) + jnp.einsum('ckz,zn->ckn', imag_part, cos_z, precision=high)
        hyb_real = hyb_real.astype(jnp.bfloat16).astype(jnp.float32)
        hyb_imag = hyb_imag.astype(jnp.bfloat16).astype(jnp.float32)
        cos_y = ky_cosine.astype(jnp.float32)
        sin_y = ky_sine.astype(jnp.float32)
        img_real = jnp.einsum('nk,ckz->cnz', cos_y, hyb_real, precision=high) - jnp.einsum('nk,ckz->cnz', sin_y, hyb_imag, precision=high)
        img_imag = jnp.einsum('nk,ckz->cnz', sin_y, hyb_real, precision=high) + jnp.einsum('nk,ckz->cnz', cos_y, hyb_imag, precision=high)
        out_real = lax.optimization_barrier(jnp.sum(maps[0] * img_real + maps[1] * img_imag, axis=0))
        out_imag = lax.optimization_barrier(jnp.sum(maps[0] * img_imag - maps[1] * img_real, axis=0))
        return jnp.stack([out_real, out_imag])
    stacked = lax.map(recon_one, jnp.arange(RO, dtype=jnp.int32))
    return jnp.transpose(stacked, (1, 0, 2, 3))
```

```python
import math

import jax
import jax.numpy as jnp
import numpy as np
from jax import lax
from jax.experimental import pallas as pl
from jax.experimental.pallas import tpu as pltpu
from jax.sharding import PartitionSpec as P

MESH = pl.DeviceIdType.MESH
BF16 = jnp.bfloat16
F32 = jnp.float32

NRO = 32
NX = 4
C = 8
LINES = 14
KY = 448
KZ = 320
ROWS = KY // 8
CROWS = 2 * LINES
MROWS = C * CROWS
WIN = 32


def dft_tables(length):
    index = np.arange(length)
    product = (index[:, None] * index[None, :]) % length
    angle = product.astype(np.float32) * np.float32(2.0 * math.pi / length)
    factor = np.float32(1.0 / math.sqrt(length))
    return (
        (np.cos(angle) * factor).astype(BF16).astype(np.float32),
        (np.sin(angle) * factor).astype(BF16).astype(np.float32),
    )


def kz_tables():
    cos, sin = dft_tables(KZ)
    out = np.zeros((2, 4, KZ, 256), np.float32)
    for k in range(2):
        cols = slice(128 * k, 128 * k + 128)
        out[0, k, :, :128], out[0, k, :, 128:] = cos[:, cols], sin[:, cols]
        out[1, k, :, :128], out[1, k, :, 128:] = -sin[:, cols], cos[:, cols]
    for q in range(2):
        re, im = slice(64 * q, 64 * q + 64), slice(128 + 64 * q, 192 + 64 * q)
        cols = slice(256, 320)
        out[0, 2 + q, :, re], out[0, 2 + q, :, im] = cos[:, cols], sin[:, cols]
        out[1, 2 + q, :, re], out[1, 2 + q, :, im] = -sin[:, cols], cos[:, cols]
    return out.astype(BF16)


def ky_tables():
    out = np.zeros((4, KY, 2, 8, 16), np.float32)
    for t, table in enumerate(dft_tables(KY)):
        out[:, :, t, :, :LINES] = table.reshape(KY, 4, 8, LINES).transpose(1, 0, 2, 3)
    return out.reshape(4, KY, 256).astype(BF16)


def partner(t):
    return ((t >> 1) & 3) | ((1 - (t & 1)) << 2) | ((t >> 3) << 3)


def dot(a, b):
    return jnp.dot(a, b, preferred_element_type=F32)


def kernel(
    ks, sens, sampled, pole_y, order_y, pole_z, order_z, kz_tab, ky_tab,
    out,
    kbuf, sraw, smp, py, oy, pz, oz, gtab, ctab,
    wgt, filt, relay, send, send2, recv, recv2, st, st2, wmat, acc, acc2,
    got_a, got_a2, part, part2, got_b, got_b2,
    ksem, lsem, ssem, rsem, sa, ra, sb, rb,
):
    ro = lax.axis_index("ro")
    coil = lax.axis_index("coil")
    x = lax.rem(coil, NX)
    zh = lax.div(coil, NX)

    small = [
        pltpu.make_async_copy(s, d, lsem.at[i])
        for i, (s, d) in enumerate(
            ((sampled, smp), (pole_y, py), (order_y, oy), (pole_z, pz), (order_z, oz))
        )
    ]
    for cp in small:
        cp.start()
    load_g = pltpu.make_async_copy(kz_tab, gtab, lsem.at[5])
    load_k = [
        pltpu.make_async_copy(ks.at[:, c], kbuf.at[:, c], ksem.at[c]) for c in range(C)
    ]
    load_k[0].start()
    load_g.start()
    for c in range(1, C):
        load_k[c].start()
    load_c = pltpu.make_async_copy(ky_tab, ctab, lsem.at[6])
    load_s = pltpu.make_async_copy(sens, sraw, lsem.at[7])
    load_c.start()
    load_s.start()

    barrier = pltpu.get_barrier_semaphore()
    for e in range(1, NRO):
        pl.semaphore_signal(
            barrier, inc=1, device_id={"ro": lax.bitwise_xor(ro, e)}, device_id_type=MESH
        )
    for i in range(1, NX):
        pl.semaphore_signal(
            barrier,
            inc=1,
            device_id={"coil": zh * NX + lax.rem(x + i, NX)},
            device_id_type=MESH,
        )
    pl.semaphore_signal(
        barrier, inc=1, device_id={"coil": (1 - zh) * NX + x}, device_id_type=MESH
    )

    for cp in small:
        cp.wait()
    first = ro * LINES
    lane = lax.broadcasted_iota(jnp.int32, (NRO, KY), 1)
    col = lax.broadcasted_iota(jnp.int32, (NRO, KZ), 1)
    freq_z = jnp.minimum(col, KZ - col).astype(F32)

    def power(quotient, order):
        square = quotient * quotient
        fourth = square * square
        return jnp.where(
            order == 1, square, jnp.where(order == 2, fourth, fourth * square)
        )

    def weigh(j, carry):
        ky = first + j
        freq_y = jnp.minimum(ky, KY - ky).astype(F32)
        here = lane == ky

        def column(ref):
            picked = jnp.where(here, ref[...].astype(F32), 0.0)
            return jnp.sum(picked, axis=1, keepdims=True)

        on = column(smp)
        wy = on / (1.0 + power(freq_y / py[...].astype(F32), oy[...]))
        pole, order = column(pz), column(oz)
        wz = 1.0 / (
            1.0 + power(freq_z / pole, jnp.broadcast_to(order, (NRO, KZ)).astype(jnp.int32))
        )
        wgt[j] = wy * wz
        return carry

    lax.fori_loop(0, LINES, weigh, 0)
    load_g.wait()

    def rows_out(c, value):
        for p in range(2):
            at = pl.multiple_of((2 * c + p) * KY, KY)
            relay[pl.ds(at, KY), :] = value[:, 128 * p : 128 * p + 128]

    def spread(block, at):
        def one(r, carry):
            block[r, at : at + 4 * CROWS, :] = relay[
                pl.ds(r, 4 * CROWS, stride=NRO), :
            ].astype(BF16)
            return carry

        lax.fori_loop(0, NRO, one, 0)

    def send_all(src, dst, k, rows):
        def one(t, carry):
            e = partner(t)

            @pl.when(e != 0)
            def _():
                d = lax.bitwise_xor(ro, e)
                pltpu.make_async_remote_copy(
                    src_ref=src.at[d, rows],
                    dst_ref=dst.at[ro, rows],
                    send_sem=ssem.at[k],
                    recv_sem=rsem.at[k],
                    device_id={"ro": d},
                    device_id_type=MESH,
                ).start()

            return carry

        lax.fori_loop(0, NRO, one, 0)
        pltpu.make_async_copy(src.at[ro, rows], dst.at[ro, rows], rsem.at[k]).start()

    for k in range(2):
        for q in range(2):

            def transform(a, carry):
                c = 4 * q + a
                if k == 0:
                    pltpu.make_async_copy(ks.at[:, c], kbuf.at[:, c], ksem.at[c]).wait()
                    for p in range(2):
                        filt[c, p] = (
                            (kbuf[p, c].astype(F32) * wgt[...])
                            .astype(BF16)
                            .reshape(LINES * NRO, KZ)
                        )
                rows_out(a, dot(filt[c, 0], gtab[0, k]) + dot(filt[c, 1], gtab[1, k]))
                return carry

            lax.fori_loop(0, 4, transform, 0)
            spread(send.at[k], 4 * CROWS * q)
            if k == 0 and q == 0:
                pl.semaphore_wait(barrier, NRO - 1 + NX)
            send_all(send.at[k], recv.at[k], k, pl.ds(4 * CROWS * q, 4 * CROWS))

    def transform2(a, carry):
        rows_out(
            a,
            dot(filt[a, 0], gtab[0, 2])
            + dot(filt[a, 1], gtab[1, 2])
            + dot(filt[4 + a, 0], gtab[0, 3])
            + dot(filt[4 + a, 1], gtab[1, 3]),
        )
        return carry

    lax.fori_loop(0, 4, transform2, 0)
    spread(send2, 0)
    send_all(send2, recv2, 2, pl.ds(0, 4 * CROWS))

    load_c.wait()
    row = lax.broadcasted_iota(jnp.int32, (256, 256), 0)
    colw = lax.broadcasted_iota(jnp.int32, (256, 256), 1)
    same = ((row >> 4) & 7) == (colw >> 5)
    is_sin = (row >> 7) == 1
    line = row & 15
    for e in range(2):
        within = (colw & 31) - 4 * e
        hit = same & (line < LINES)
        real = hit & (within == line)
        imag = hit & (within - LINES == line)
        sel0 = jnp.where(is_sin, -jnp.where(imag, 1.0, 0.0), jnp.where(real, 1.0, 0.0))
        sel1 = jnp.where(is_sin, jnp.where(real, 1.0, 0.0), jnp.where(imag, 1.0, 0.0))
        for g in range(4):
            at = slice(256 * g, 256 * g + 256)
            wmat[e, 0:KY, at] = dot(ctab[g], sel0.astype(BF16)).astype(BF16)
            wmat[e, KY : 2 * KY, at] = dot(ctab[g], sel1.astype(BF16)).astype(BF16)

    load_s.wait()
    eye = (
        lax.broadcasted_iota(jnp.int32, (KY, KY), 0)
        == lax.broadcasted_iota(jnp.int32, (KY, KY), 1)
    )
    eye = jnp.where(eye, 1.0, 0.0).astype(BF16)

    def flip(value):
        return lax.dot_general(
            eye, value, (((1,), (1,)), ((), ())), preferred_element_type=F32
        ).astype(BF16)

    for p in range(2):

        def turn(c, carry):
            st[p, c] = flip(sraw[p, c, 0:256, :])
            return carry

        lax.fori_loop(0, C, turn, 0)

        def turn2(a, carry):
            both = jnp.concatenate(
                [sraw[p, a, 256:KZ, :], sraw[p, 4 + a, 256:KZ, :]], axis=0
            )
            st2[p, a] = flip(both)
            return carry

        lax.fori_loop(0, 4, turn2, 0)

    def window(ref, c):
        at = CROWS * c - 4 * (c % 2)
        return ref[:, at : at + WIN, :].reshape(NRO * WIN, 128)

    def combine(maps, images):
        re = im = None
        for (sr, si), (xr, xi) in zip(maps, images):
            sr, si = sr.astype(F32), si.astype(F32)
            a, b = sr * xr + si * xi, sr * xi - si * xr
            re, im = (a, b) if re is None else (re + a, im + b)
        return re, im

    def ky_pair(ref, e, c0, c1):
        both = jnp.concatenate([window(ref, c0), window(ref, c1)], axis=1)
        value = dot(wmat[e], both)
        return [
            (value[0:KY, 128 * i : 128 * i + 128], value[KY:, 128 * i : 128 * i + 128])
            for i in range(2)
        ]

    def reduce_x(src, dst, k):
        for i in range(1, NX):
            there = lax.rem(x + i, NX)
            pltpu.make_async_remote_copy(
                src_ref=src.at[:, there],
                dst_ref=dst.at[i - 1],
                send_sem=sa.at[k],
                recv_sem=ra.at[k],
                device_id={"coil": zh * NX + there},
                device_id_type=MESH,
            ).start()

    def reduce_z(src, got, total, dst, k):
        pltpu.make_async_copy(got, got, ra.at[k]).wait()
        total[...] = src[:, x] + got[0] + got[1] + got[2]
        pltpu.make_async_remote_copy(
            src_ref=total.at[1 - zh],
            dst_ref=dst,
            send_sem=sb.at[k],
            recv_sem=rb.at[k],
            device_id={"coil": (1 - zh) * NX + x},
            device_id_type=MESH,
        ).start()

    for k in range(2):
        pltpu.make_async_copy(send.at[k], recv.at[k], rsem.at[k]).wait()
        cols = slice(128 * k, 128 * k + 128)
        begun = False
        for e in range(2):
            for m in range(2):
                pair = (4 * m + e, 4 * m + e + 2)
                images = ky_pair(recv.at[k], e, *pair)
                maps = [(st[0, c, :, cols], st[1, c, :, cols]) for c in pair]
                parts = combine(maps, images)
                for g in range(8):
                    for p in range(2):
                        v = parts[p][ROWS * g : ROWS * g + ROWS]
                        if begun:
                            v = v + acc[k, g // NX, g % NX, p]
                        acc[k, g // NX, g % NX, p] = v
                begun = True
        reduce_x(acc.at[k], got_a.at[k], k)
        reduce_z(acc.at[k], got_a.at[k], part.at[k], got_b.at[k], k)

    pltpu.make_async_copy(send2, recv2, rsem.at[2]).wait()
    re = im = None
    for e in range(2):
        images = ky_pair(recv2, e, e, e + 2)
        maps = [(st2[0, a], st2[1, a]) for a in (e, e + 2)]
        a, b = combine(maps, images)
        re, im = (a, b) if re is None else (re + a, im + b)
    low = lax.broadcasted_iota(jnp.int32, (KY, 128), 1) < 64
    both = jnp.where(
        low, re + pltpu.roll(re, 64, 1), im + pltpu.roll(im, 64, 1)
    )
    for g in range(8):
        acc2[g // NX, g % NX] = both[ROWS * g : ROWS * g + ROWS]
    reduce_x(acc2, got_a2, 2)
    reduce_z(acc2, got_a2, part2, got_b2, 2)

    for k in range(2):
        pltpu.make_async_copy(got_b.at[k], got_b.at[k], rb.at[k]).wait()
        out[:, :, 128 * k : 128 * k + 128] = part[k, zh] + got_b[k]
    pltpu.make_async_copy(got_b2, got_b2, rb.at[2]).wait()
    last = part2[zh] + got_b2[...]
    out[0, :, 256:KZ] = last[:, 0:64]
    out[1, :, 256:KZ] = last[:, 64:128]

    for k in range(2):
        sent = send.at[k, pl.ds(0, NRO - 1)]
        pltpu.make_async_copy(sent, sent, ssem.at[k]).wait()
        pltpu.make_async_copy(got_a.at[k], got_a.at[k], sa.at[k]).wait()
        pltpu.make_async_copy(got_b.at[k], got_b.at[k], sb.at[k]).wait()
    sent = send2.at[pl.ds(0, NRO - 1)]
    pltpu.make_async_copy(sent, sent, ssem.at[2]).wait()
    pltpu.make_async_copy(got_a2, got_a2, sa.at[2]).wait()
    pltpu.make_async_copy(got_b2, got_b2, sb.at[2]).wait()


def on_device(kspace, sensitivity, sampled, pole_y, order_y, pole_z, order_z):
    lines_first = jnp.transpose(kspace, (0, 1, 3, 2, 4))
    maps = jnp.transpose(sensitivity[:, :, 0], (0, 1, 3, 2))
    vmem, dma = pltpu.VMEM, pltpu.SemaphoreType.DMA
    anywhere = pl.BlockSpec(memory_space=pl.ANY)
    image = pl.pallas_call(
        kernel,
        out_shape=jax.ShapeDtypeStruct((2, ROWS, KZ), F32),
        in_specs=[anywhere] * 9,
        out_specs=pl.BlockSpec(memory_space=pltpu.VMEM),
        scratch_shapes=[
            vmem((2, C, LINES, NRO, KZ), BF16),
            vmem((2, C, KZ, KY), BF16),
            vmem((NRO, KY), jnp.int32),
            vmem((NRO, KZ), jnp.int32),
            vmem((NRO, KZ), jnp.int32),
            vmem((NRO, KY), jnp.int32),
            vmem((NRO, KY), jnp.int32),
            vmem((2, 4, KZ, 256), BF16),
            vmem((4, KY, 256), BF16),
            vmem((LINES, NRO, KZ), F32),
            vmem((C, 2, LINES * NRO, KZ), BF16),
            vmem((4 * CROWS * NRO, 128), F32),
            vmem((2, NRO, MROWS, 128), BF16),
            vmem((NRO, 4 * CROWS, 128), BF16),
            vmem((2, NRO, MROWS, 128), BF16),
            vmem((NRO, 4 * CROWS, 128), BF16),
            vmem((2, C, KY, 256), BF16),
            vmem((2, 4, KY, 128), BF16),
            vmem((2, 2 * KY, NRO * WIN), BF16),
            vmem((2, 2, NX, 2, ROWS, 128), F32),
            vmem((2, NX, ROWS, 128), F32),
            vmem((2, NX - 1, 2, 2, ROWS, 128), F32),
            vmem((NX - 1, 2, ROWS, 128), F32),
            vmem((2, 2, 2, ROWS, 128), F32),
            vmem((2, ROWS, 128), F32),
            vmem((2, 2, ROWS, 128), F32),
            vmem((ROWS, 128), F32),
            dma((C,)),
            dma((8,)),
            dma((3,)),
            dma((3,)),
            dma((3,)),
            dma((3,)),
            dma((3,)),
            dma((3,)),
        ],
        compiler_params=pltpu.CompilerParams(
            collective_id=0, has_side_effects=True, vmem_limit_bytes=60 * 2**20
        ),
    )(
        lines_first, maps, sampled, pole_y, order_y, pole_z, order_z,
        jnp.asarray(kz_tables()), jnp.asarray(ky_tables()),
    )
    return image[:, None]


def solution(mesh):
    return jax.shard_map(
        on_device,
        mesh=mesh,
        in_specs=(
            P(None, "coil", None, "ro", None),
            P(None, "coil", "ro", None, None),
            P(),
            P(),
            P(),
            P(),
            P(),
        ),
        out_specs=P(None, "ro", "coil", None),
        check_vma=False,
    )
```
